128 devices in a mesh: row: 16 (over y_hi, z, core), col: 8 (over x, y_lo).
Axes of the slice: x: 4, y: 4 (y_hi: 2, y_lo: 2; y = y_hi * 2 + y_lo), z: 4, core: 2. Of those that a mesh axis runs over, the one named last changes fastest.
Arguments:
- amplitudes: float32 [16, 16, 160, 160], P('row', 'col'), may hold values from -8 to 8, as said below
- vvvv: float32 [160, 160, 160, 160], P('row', None, 'col'), may hold values from -0.0390625 to 0.0390625
- hole_ints: float32 [16, 16, 16, 16], replicated, may hold values from -0.375 to 0.375
- exchange_ints: float32 [16, 16, 160, 160], P('row', None, 'col'), may hold values from -0.0024414062 to 0.0024414062
- fock_occ: float32 [16, 16], replicated, may hold values from -1.5 to 1.5
- fock_vir: float32 [160, 160], replicated, may hold values from -0.5 to 0.5
- eps_occ: float32 [16], replicated, may hold values from -2 to -0.5
- eps_vir: float32 [160], replicated, may hold values from 0.3 to 3
Outputs:
- update: float32 [16, 16, 160, 160], P('row', 'col')
The draws below stay inside these ranges and needn't reach their ends.
Inputs may be any that keep to these rules, and one draw needn't show every extreme that they name: amplitudes[i, j, a, b] equals amplitudes[j, i, b, a].
All inputs are finite; a program needn't handle non-finite values.
Results may differ from the reference program's by a relative error of at most 0.000064.
Values sent between devices are 32-bit elements; how exact they have to be, the bound alone decides.
No kernel may reach another device: no remote copies, remote signals or barrier semaphores. Data moves between devices by JAX's collectives and lax.ppermute only.
A program may use at most 128 MiB of HBM per device.

```python
import jax
import jax.numpy as jnp
from jax import lax

NO = 16
NV = 160


def draw_amplitudes(key, part):
    first_key = jax.random.fold_in(key, 11)
    initial = jax.random.normal(first_key, (NO, NO, NV, NV), jnp.float32)
    symmetric = (initial + initial.transpose(1, 0, 3, 2)) * 0.7071
    return jnp.clip(symmetric, -8.0, 8.0)


def shard_levels(key, dims, shards, least, high):
    loudness = 1.0
    for dim, blocks in shards:
        draws = jax.random.uniform(jax.random.fold_in(jax.random.fold_in(key, 6), dim), (blocks,), jnp.float32, least / len(shards), high / len(shards))
        loudness = loudness * jnp.repeat(jnp.exp(draws), dims[dim] // blocks).reshape((-1,) + (1,) * (len(dims) - 1 - dim))
    return loudness


def centred(stream_key, extent, scale, bound, pieces=(), dtype=jnp.bfloat16):
    gain = shard_levels(stream_key, extent, pieces, -0.22, 0.18) if pieces else 1.0
    array = jax.random.normal(stream_key, extent, jnp.float32) * scale * gain
    return jnp.minimum(jnp.maximum(array, -bound), bound).astype(dtype)


def setup_inputs(seed: int = 0) -> dict:
    keys = jax.random.split(jax.random.key(seed), 9)
    amplitudes = draw_amplitudes(jax.random.fold_in(keys[8], 71), 0)
    vvvv = centred(keys[1], (NV, NV, NV, NV), (NV * NV) ** -0.5, 0.0390625, ((0, 16), (2, 8)), jnp.float32)
    hole_ints = centred(keys[2], (NO, NO, NO, NO), (NO * NO) ** -0.5, 0.375, (), jnp.float32)
    exchange_ints = centred(keys[3], (NO, NO, NV, NV), (NO * NO * NV * NV) ** -0.5, 0.0024414062, ((0, 16), (2, 8)), jnp.float32)
    fock_occ = centred(keys[4], (NO, NO), NO ** -0.5, 1.5, (), jnp.float32)
    fock_vir = centred(keys[5], (NV, NV), NV ** -0.5, 0.5, (), jnp.float32)
    eps_occ = jnp.clip(jax.random.uniform(keys[6], (NO,), jnp.float32, -2.0, -0.5), -2.0, -0.5)
    eps_vir = jnp.clip(jax.random.uniform(keys[7], (NV,), jnp.float32, 0.3, 3.0), 0.3, 3.0)
    return {"amplitudes": amplitudes, "vvvv": vvvv, "hole_ints": hole_ints, "exchange_ints": exchange_ints, "fock_occ": fock_occ, "fock_vir": fock_vir, "eps_occ": eps_occ, "eps_vir": eps_vir}


def reference(amplitudes, vvvv, hole_ints, exchange_ints, fock_occ, fock_vir, eps_occ, eps_vir):
    highest = lax.Precision.HIGHEST
    matrix = amplitudes.reshape(NO * NO, NV * NV)
    ladder = lax.dot_general(matrix, vvvv.reshape(NV * NV, NV * NV), (((1,), (1,)), ((), ())), precision=highest)
    quadratic = lax.dot_general(matrix, exchange_ints.reshape(NO * NO, NV * NV), (((1,), (1,)), ((), ())), precision=highest)
    chi = hole_ints.reshape(NO * NO, NO * NO).T + quadratic
    hole = jnp.dot(chi, matrix, precision=highest)
    occupied_term = jnp.einsum("ikx,kj->ijx", amplitudes.reshape(NO, NO, NV * NV), fock_occ, precision=highest).reshape(NO * NO, NV * NV)
    raw = (ladder + hole - occupied_term).reshape(NO, NO, NV, NV)
    total = raw + raw.transpose(1, 0, 3, 2)
    total = total + jnp.einsum("ijac,cb->ijab", amplitudes, fock_vir, precision=highest)
    total = total + jnp.einsum("ac,ijcb->ijab", fock_vir, amplitudes, precision=highest)
    denominator = eps_occ[:, None, None, None] + eps_occ[None, :, None, None] - eps_vir[None, None, :, None] - eps_vir[None, None, None, :]
    return total / denominator
```

```python
import functools

import jax
import jax.numpy as jnp
from jax import lax
from jax.experimental import pallas as pl
from jax.experimental.pallas import tpu as pltpu
from jax.sharding import PartitionSpec as P

NO = 16
NV = 160
ROWS = 16
COLS = 8
AB = NV // ROWS
CB = NV // COLS
KT = 25
VROWS = AB * NV
EROWS = AB * 4
MROWS = VROWS + NO + EROWS
NT = (((1,), (1,)), ((), ()))


def row_perm(dy, dz, dc):
    def source(r):
        return ((r // 8 + dy) % 2) * 8 + ((r // 2 + dz) % 4) * 2 + ((r % 2) ^ dc)

    return [(source(r), r) for r in range(ROWS)]


def pack_kernel(t_ref, o_ref, tail):
    tail[:, :, 0:32] = t_ref[:, :, 128:NV]
    for c in range(COLS):
        for j in range(2):
            o_ref[c, j, 0:CB, :] = t_ref[j, c * CB : (c + 1) * CB, 0:128]
            tails = [
                tail[j, pl.ds(c * CB + cc, CB // 4, stride=4), :][:, 0:32] for cc in range(4)
            ]
            o_ref[c, j, CB:KT, :] = jnp.concatenate(tails, axis=1)


def pack(t):
    return pl.pallas_call(
        pack_kernel,
        out_shape=jax.ShapeDtypeStruct((COLS, 2, KT, 128), jnp.float32),
        scratch_shapes=[pltpu.VMEM((2, NV, 128), jnp.float32)],
        cost_estimate=pl.CostEstimate(flops=0, bytes_accessed=600000, transcendentals=0),
    )(t)


def split(x):
    hi = x.astype(jnp.bfloat16)
    lo = (x - hi.astype(jnp.float32)).astype(jnp.bfloat16)
    return hi, lo


def ladder_kernel(
    tbl_ref, s_ref, q_ref, v_ref, k_ref, e_ref, l_ref, chi_ref, p_ref, hi, lo, ghi, glo, acc, pacc
):
    step = pl.program_id(0)
    for rel in range(ROWS):
        ref = s_ref if rel < 8 else q_ref
        start = pl.multiple_of(tbl_ref[rel] * NO, NO)
        for kt in range(5):
            index = step * 4 + kt if kt < 4 else CB + step
            ph, plo = split(ref[rel % 8, index])
            ghi[pl.ds(start, NO), kt * 128 : (kt + 1) * 128] = ph
            glo[pl.ds(start, NO), kt * 128 : (kt + 1) * 128] = plo
    for a in range(AB + 1):
        rows = NV if a < AB else NO
        base = a * NV

        def get(cc, lanes, a=a):
            return v_ref[a, cc, :, lanes] if a < AB else k_ref[cc, :, lanes]

        for kt in range(5):
            if kt < 4:
                x = get(kt, slice(0, 128))
            else:
                x = jnp.concatenate([get(cc, slice(128, NV)) for cc in range(4)], axis=1)
            xh, xl = split(x)
            hi[base : base + rows, kt * 128 : (kt + 1) * 128] = xh
            lo[base : base + rows, kt * 128 : (kt + 1) * 128] = xl

    dot = functools.partial(
        lax.dot_general, dimension_numbers=NT, preferred_element_type=jnp.float32
    )
    part = dot(hi[...], ghi[...]) + dot(hi[...], glo[...]) + dot(lo[...], ghi[...])

    @pl.when(step == 0)
    def _():
        acc[...] = part

    @pl.when(step > 0)
    def _():
        acc[...] += part

    pacc[step] = dot(e_ref[...], ghi[...]) + dot(e_ref[...], glo[...])

    @pl.when(step == pl.num_programs(0) - 1)
    def _():
        for a in range(AB):
            for c in range(COLS):
                first = a * NV + c * CB
                l_ref[c, a * CB : (a + 1) * CB, :] = acc[first : first + CB, :]
            for g in range(5):
                p_ref[a * CB + g * 4 : a * CB + g * 4 + 4, :] = pacc[g, a * 4 : a * 4 + 4, :]
        chi_ref[...] = acc[VROWS : VROWS + NO, :]


def ladder(tbl, s, q, v, k, e):
    whole = lambda shape: pl.BlockSpec(shape, lambda g, t: (0,) * len(shape))
    return pl.pallas_call(
        ladder_kernel,
        out_shape=(
            jax.ShapeDtypeStruct((COLS, AB * CB, NO * NO), jnp.float32),
            jax.ShapeDtypeStruct((NO, NO * NO), jnp.float32),
            jax.ShapeDtypeStruct((AB * CB, NO * NO), jnp.float32),
        ),
        grid_spec=pltpu.PrefetchScalarGridSpec(
            num_scalar_prefetch=1,
            grid=(5,),
            in_specs=[
                whole((8, KT, NO, 128)),
                whole((8, KT, NO, 128)),
                pl.BlockSpec((AB, 4, NV, NV), lambda g, t: (0, g, 0, 0)),
                pl.BlockSpec((4, NO, NV), lambda g, t: (g, 0, 0)),
                whole((EROWS, 640)),
            ],
            out_specs=(
                whole((COLS, AB * CB, NO * NO)),
                whole((NO, NO * NO)),
                whole((AB * CB, NO * NO)),
            ),
            scratch_shapes=[
                pltpu.VMEM((VROWS + NO, 640), jnp.bfloat16),
                pltpu.VMEM((VROWS + NO, 640), jnp.bfloat16),
                pltpu.VMEM((NO * NO, 640), jnp.bfloat16),
                pltpu.VMEM((NO * NO, 640), jnp.bfloat16),
                pltpu.VMEM((VROWS + NO, NO * NO), jnp.float32),
                pltpu.VMEM((5, EROWS, NO * NO), jnp.float32),
            ],
        ),
        compiler_params=pltpu.CompilerParams(vmem_limit_bytes=48 << 20),
        cost_estimate=pl.CostEstimate(
            flops=3 * 2 * 1680 * 3200 * 256, bytes_accessed=38 << 20, transcendentals=0
        ),
    )(tbl, s, q, v, k, e)


def final_kernel(e_ref, x_ref, tf_ref, vrow_ref, vcol_ref, o_ref, left, right):
    for o in range(2):
        for s in range(2):
            for a in range(AB):
                pieces = [x_ref[o, s, c, :, a * CB : (a + 1) * CB] for c in range(COLS)]
                line = jnp.concatenate(pieces, axis=1)
                left[o, s, pl.ds(a, ROWS, stride=AB), :] = line[:, 0:128]
                right[o, s, pl.ds(a, ROWS, stride=AB), 0:32] = line[:, 128:NV]
    for s in range(2):
        full = [
            jnp.concatenate([left[o, s], right[o, s, :, 0:32]], axis=1) for o in range(2)
        ]
        total = full[0] + full[1].T + tf_ref[s]
        den = (e_ref[s] - vcol_ref[...]) - vrow_ref[...]
        o_ref[s] = total / den


def finish(e, x, tf, eps_vir):
    return pl.pallas_call(
        final_kernel,
        out_shape=jax.ShapeDtypeStruct((2, NV, NV), jnp.float32),
        in_specs=[pl.BlockSpec(memory_space=pltpu.SMEM)]
        + [pl.BlockSpec(memory_space=pltpu.VMEM)] * 4,
        out_specs=pl.BlockSpec(memory_space=pltpu.VMEM),
        scratch_shapes=[pltpu.VMEM((2, 2, NV, 128), jnp.float32)] * 2,
        cost_estimate=pl.CostEstimate(flops=0, bytes_accessed=2 << 20, transcendentals=0),
    )(e, x, tf, eps_vir.reshape(1, NV), eps_vir.reshape(NV, 1))


def on_device(amplitudes, vvvv, hole_ints, exchange_ints, fock_occ, fock_vir, eps_occ, eps_vir):
    high = lax.Precision.HIGHEST
    row = lax.axis_index("row")
    col = lax.axis_index("col")
    t = amplitudes[0]
    packed = pack(t)
    arrived = lax.all_to_all(packed, "col", split_axis=0, concat_axis=0, tiled=True)
    x = arrived.reshape(NO, KT, 128).transpose(1, 0, 2)

    pair = jnp.stack([x, lax.ppermute(x, "row", row_perm(1, 0, 0))])
    rings = [pair] + [lax.ppermute(pair, "row", row_perm(0, dz, 0)) for dz in (1, 2, 3)]
    own = jnp.stack(rings)
    other = lax.ppermute(own, "row", row_perm(0, 0, 1))
    own = own.reshape(8, KT, NO, 128)
    other = other.reshape(8, KT, NO, 128)

    rel = jnp.arange(ROWS, dtype=jnp.int32)
    dc, dz, dy = rel // 8, (rel // 2) % 4, rel % 2
    table = ((row // 8 + dy) % 2) * 8 + ((row // 2 + dz) % 4) * 2 + ((row % 2) ^ dc)

    e_row = jnp.arange(EROWS, dtype=jnp.int32)[:, None]
    e_col = jnp.arange(640, dtype=jnp.int32)[None, :]
    want = row * AB + e_row // 4
    cc = e_row % 4
    place = jnp.where(want < 128, cc * 128 + want, 512 + cc * 32 + want - 128)
    onehot = (e_col == place).astype(jnp.bfloat16)

    lad, chi_part, block = ladder(
        table,
        own,
        other,
        vvvv.transpose(0, 2, 1, 3),
        exchange_ints[0].transpose(1, 0, 2),
        onehot,
    )
    scattered = lax.all_to_all(lad, "col", split_axis=0, concat_axis=0, tiled=True)
    summed = jnp.sum(scattered, axis=0)

    chi_cols = jnp.sum(lax.all_gather(chi_part, "col", axis=0), axis=0)
    chi_rows = lax.all_gather(chi_cols, "row", axis=0)
    eye = jnp.eye(NO, dtype=jnp.float32)
    fixed = hole_ints - eye[:, None, :, None] * fock_occ[None, :, None, :]
    chi = fixed + chi_rows.reshape(NO, NO, NO, NO)
    chi = chi.transpose(1, 0, 2, 3).reshape(NO * NO, NO * NO)
    raw = summed + jnp.dot(block, chi, precision=high)
    raw = jnp.pad(raw.T, ((0, 0), (0, 256 - AB * CB))).reshape(NO, NO, 256)
    sending = jnp.stack([raw, raw.transpose(1, 0, 2)])
    sending = sending.reshape(2, NO, COLS, 2, 256).transpose(1, 2, 0, 3, 4)
    sending = sending.reshape(ROWS * COLS, 4, 256)
    back = lax.all_to_all(sending, ("row", "col"), split_axis=0, concat_axis=0, tiled=True)
    back = back.reshape(ROWS, COLS, 2, 2, 256).transpose(2, 3, 1, 0, 4)

    tf = jnp.einsum("jac,cb->jab", t, fock_vir, precision=high)
    tf = tf + jnp.einsum("ac,jcb->jab", fock_vir, t, precision=high)
    first = lax.dynamic_slice_in_dim(eps_occ, row, 1)
    second = lax.dynamic_slice_in_dim(eps_occ, col * 2, 2)
    return finish(first + second, back, tf, eps_vir)[None]


def solution(mesh):
    in_specs = (
        P("row", "col", None, None),
        P("row", None, "col", None),
        P(),
        P("row", None, "col", None),
        P(),
        P(),
        P(),
        P(),
    )
    return jax.shard_map(
        on_device,
        mesh=mesh,
        in_specs=in_specs,
        out_specs=P("row", "col", None, None),
        check_vma=False,
    )
```

```python
import functools

import jax
import jax.numpy as jnp
from jax import lax
from jax.experimental import pallas as pl
from jax.experimental.pallas import tpu as pltpu
from jax.sharding import PartitionSpec as P

NO = 16
NV = 160
ROWS = 16
COLS = 8
AB = NV // ROWS
CB = NV // COLS
KT = 25
VROWS = AB * NV
EROWS = AB * 4
HALF = VROWS // 2
NT = (((1,), (1,)), ((), ()))
VMEM = pl.BlockSpec(memory_space=pltpu.VMEM)


def row_perm(dy, dz, dc):
    def source(r):
        return ((r // 8 + dy) % 2) * 8 + ((r // 2 + dz) % 4) * 2 + ((r % 2) ^ dc)

    return [(source(r), r) for r in range(ROWS)]


def pack_kernel(t_ref, o_ref, tail):
    tail[:, :, 0:32] = t_ref[:, :, 128:NV]
    for c in range(COLS):
        for j in range(2):
            o_ref[c, j, 0:CB, :] = t_ref[j, c * CB : (c + 1) * CB, 0:128]
            tails = [
                tail[j, pl.ds(c * CB + cc, CB // 4, stride=4), :][:, 0:32] for cc in range(4)
            ]
            o_ref[c, j, CB:KT, :] = jnp.concatenate(tails, axis=1)


def pack(t):
    return pl.pallas_call(
        pack_kernel,
        out_shape=jax.ShapeDtypeStruct((COLS, 2, KT, 128), jnp.float32),
        scratch_shapes=[pltpu.VMEM((2, NV, 128), jnp.float32)],
        cost_estimate=pl.CostEstimate(flops=0, bytes_accessed=600000, transcendentals=0),
    )(t)


def split(x):
    hi = x.astype(jnp.bfloat16)
    lo = (x - hi.astype(jnp.float32)).astype(jnp.bfloat16)
    return hi, lo


def prepare_kernel(tbl_ref, s_ref, q_ref, k_ref, ghi, glo, chi_ref):
    for rel in range(ROWS):
        ref = s_ref if rel < 8 else q_ref
        start = pl.multiple_of(tbl_ref[rel] * NO, NO)
        for kt in range(KT):
            g, place = (kt // 4, kt % 4) if kt < CB else (kt - CB, 4)
            hi, lo = split(ref[rel % 8, kt])
            ghi[g, pl.ds(start, NO), place * 128 : (place + 1) * 128] = hi
            ghi[g, pl.ds(start, NO), 640 + place * 128 : 640 + (place + 1) * 128] = hi
            glo[g, pl.ds(start, NO), place * 128 : (place + 1) * 128] = lo
    chi = jnp.zeros((NO * NO, NO), jnp.float32)
    for g in range(5):
        parts = [k_ref[g * 4 + cc, :, 0:128] for cc in range(4)]
        parts.append(
            jnp.concatenate([k_ref[g * 4 + cc, :, 128:NV] for cc in range(4)], axis=1)
        )
        hi, lo = split(jnp.concatenate(parts, axis=1))
        chi = chi + dot_nt(ghi[g, :, 0:640], hi) + dot_nt(ghi[g, :, 0:640], lo)
        chi = chi + dot_nt(glo[g], hi)
    chi_ref[...] = chi.T


def dot_nt(x, y):
    return lax.dot_general(x, y, NT, preferred_element_type=jnp.float32)


def prepare(tbl, s, q, k):
    return pl.pallas_call(
        prepare_kernel,
        out_shape=(
            pltpu.VMEM((5, NO * NO, 1280), jnp.bfloat16),
            pltpu.VMEM((5, NO * NO, 640), jnp.bfloat16),
            jax.ShapeDtypeStruct((NO, NO * NO), jnp.float32),
        ),
        in_specs=[pl.BlockSpec(memory_space=pltpu.SMEM)] + [VMEM] * 3,
        out_specs=(VMEM, VMEM, VMEM),
        compiler_params=pltpu.CompilerParams(vmem_limit_bytes=7 << 20),
        cost_estimate=pl.CostEstimate(flops=0, bytes_accessed=8 << 20, transcendentals=0),
    )(tbl, s, q, k)


def ladder_kernel(groups, ghi, glo, v_hbm, *refs):
    first, last = groups[0] == 0, groups[-1] == 4
    refs = list(refs)
    before = None if first else refs.pop(0)
    e_ref = refs.pop(0) if last else None
    out = refs.pop(0)
    p_ref = refs.pop(0) if last else None
    buf, hi, lo, sem = refs
    blocks = [(g, half) for g in groups for half in range(2)]
    copies = []
    for n, (g, half) in enumerate(blocks):
        source = v_hbm.at[pl.ds(half * (AB // 2), AB // 2), pl.ds(g * 4, 4)]
        copies.append(pltpu.make_async_copy(source, buf.at[n], sem.at[n]))
        copies[-1].start()
    if last:
        for g in range(5):
            block = dot_nt(e_ref[...], ghi[g, :, 0:640]) + dot_nt(e_ref[...], glo[g])
            for a in range(AB):
                row = a * CB + g * 4
                p_ref[row : row + 4, :] = block[a * 4 : a * 4 + 4, :]

    def convert(n):
        copies[n].wait()
        for a in range(AB // 2):
            rows = slice(a * NV, (a + 1) * NV)
            for kt in range(5):
                if kt < 4:
                    x = buf[n, a, kt, :, 0:128]
                else:
                    tails = [buf[n, a, cc, :, 128:NV] for cc in range(4)]
                    x = jnp.concatenate(tails, axis=1)
                xh, xl = split(x)
                hi[n, rows, kt * 128 : (kt + 1) * 128] = xh
                lo[n, rows, kt * 128 : (kt + 1) * 128] = xl

    totals = [None, None]
    if not first:
        totals = [before[0:HALF, :], before[HALF:VROWS, :]]
    for n, (g, half) in enumerate(blocks):
        convert(n)
        part = dot_nt(hi[n], ghi[g, :, 0:640]) + dot_nt(hi[n], glo[g])
        part = part + dot_nt(lo[n], ghi[g, :, 0:640])
        totals[half] = part if totals[half] is None else totals[half] + part
    for half in range(2):
        total = totals[half]
        if not last:
            out[half * HALF : (half + 1) * HALF, :] = total
            continue
        for a in range(AB // 2):
            row = (half * (AB // 2) + a) * CB
            for c in range(COLS):
                start = a * NV + c * CB
                out[c, row : row + CB, :] = total[start : start + CB, :]


def ladder(ghi, glo, v, groups, before=None, onehot=None):
    operands = [ghi, glo, v]
    in_specs = [VMEM, VMEM, pl.BlockSpec(memory_space=pltpu.HBM)]
    for extra in (before, onehot):
        if extra is not None:
            operands.append(extra)
            in_specs.append(VMEM)
    if onehot is not None:
        out_shape = (
            jax.ShapeDtypeStruct((COLS, AB * CB, NO * NO), jnp.float32),
            jax.ShapeDtypeStruct((AB * CB, NO * NO), jnp.float32),
        )
        out_specs = (VMEM, VMEM)
    else:
        out_shape = pltpu.VMEM((VROWS, NO * NO), jnp.float32)
        out_specs = VMEM
    count = 2 * len(groups)
    return pl.pallas_call(
        functools.partial(ladder_kernel, groups),
        out_shape=out_shape,
        in_specs=in_specs,
        out_specs=out_specs,
        scratch_shapes=[
            pltpu.VMEM((count, AB // 2, 4, NV, NV), jnp.float32),
            pltpu.VMEM((count, HALF, 640), jnp.bfloat16),
            pltpu.VMEM((count, HALF, 640), jnp.bfloat16),
            pltpu.SemaphoreType.DMA((count,)),
        ],
        compiler_params=pltpu.CompilerParams(vmem_limit_bytes=(6 + 13 * len(groups)) << 20),
        cost_estimate=pl.CostEstimate(
            flops=len(groups) * 3 * 2 * 1600 * 640 * 256,
            bytes_accessed=len(groups) * (8 << 20),
            transcendentals=0,
        ),
    )(*operands)


def post_kernel(tbl_ref, x_ref, chi_ref, w_ref, f_ref, p_ref, o_ref, c0, c1, r0, r1, m1):
    owner = lax.broadcasted_iota(jnp.int32, (NO, NO * NO), 1) // NO
    for rel in range(ROWS):
        k = tbl_ref[rel]
        piece = chi_ref[rel] + w_ref[pl.ds(pl.multiple_of(k * NO, NO), NO), :]
        piece = piece - jnp.where(owner == k, f_ref[...], 0.0)
        c0[pl.ds(k, NO, stride=NO), :] = piece[:, 0:128]
        c1[pl.ds(k, NO, stride=NO), :] = piece[:, 128:256]
    chi = jnp.concatenate([c0[...], c1[...]], axis=1)
    total = x_ref[0]
    for c in range(1, COLS):
        total = total + x_ref[c]
    total = total + jnp.dot(
        p_ref[...], chi, precision=lax.Precision.HIGHEST, preferred_element_type=jnp.float32
    )
    total = jnp.concatenate([total, jnp.zeros((256 - AB * CB, NO * NO), jnp.float32)], axis=0)
    raw = total.T
    r0[...] = raw[:, 0:128]
    r1[...] = raw[:, 128:256]
    for i in range(NO):
        m1[i * NO : (i + 1) * NO, 0:128] = r0[pl.ds(i, NO, stride=NO), :]
        m1[i * NO : (i + 1) * NO, 128:256] = r1[pl.ds(i, NO, stride=NO), :]
    flipped = m1[...]
    for d in range(ROWS * COLS):
        o_ref[d, 0:2, :] = raw[2 * d : 2 * d + 2, :]
        o_ref[d, 2:4, :] = flipped[2 * d : 2 * d + 2, :]


def post(tbl, scattered, chi, bare, fock, block):
    return pl.pallas_call(
        post_kernel,
        out_shape=jax.ShapeDtypeStruct((ROWS * COLS, 4, 256), jnp.float32),
        in_specs=[pl.BlockSpec(memory_space=pltpu.SMEM)] + [VMEM] * 5,
        out_specs=VMEM,
        scratch_shapes=[pltpu.VMEM((NO * NO, 128), jnp.float32)] * 4
        + [pltpu.VMEM((NO * NO, 256), jnp.float32)],
        compiler_params=pltpu.CompilerParams(vmem_limit_bytes=12 << 20),
        cost_estimate=pl.CostEstimate(
            flops=6 * 2 * 200 * 65536, bytes_accessed=3 << 20, transcendentals=0
        ),
    )(tbl, scattered, chi, bare, fock, block)


def final_kernel(e_ref, x_ref, tf_ref, vrow_ref, vcol_ref, o_ref, left, right):
    for o in range(2):
        for s in range(2):
            for a in range(AB):
                pieces = [x_ref[o, s, c, :, a * CB : (a + 1) * CB] for c in range(COLS)]
                line = jnp.concatenate(pieces, axis=1)
                left[o, s, pl.ds(a, ROWS, stride=AB), :] = line[:, 0:128]
                right[o, s, pl.ds(a, ROWS, stride=AB), 0:32] = line[:, 128:NV]
    for s in range(2):
        full = [
            jnp.concatenate([left[o, s], right[o, s, :, 0:32]], axis=1) for o in range(2)
        ]
        total = full[0] + full[1].T + tf_ref[s]
        den = (e_ref[s] - vcol_ref[...]) - vrow_ref[...]
        o_ref[s] = total / den


def finish(e, x, tf, eps_vir):
    return pl.pallas_call(
        final_kernel,
        out_shape=jax.ShapeDtypeStruct((2, NV, NV), jnp.float32),
        in_specs=[pl.BlockSpec(memory_space=pltpu.SMEM)]
        + [pl.BlockSpec(memory_space=pltpu.VMEM)] * 4,
        out_specs=pl.BlockSpec(memory_space=pltpu.VMEM),
        scratch_shapes=[pltpu.VMEM((2, 2, NV, 128), jnp.float32)] * 2,
        cost_estimate=pl.CostEstimate(flops=0, bytes_accessed=2 << 20, transcendentals=0),
    )(e, x, tf, eps_vir.reshape(1, NV), eps_vir.reshape(NV, 1))


def on_device(amplitudes, vvvv, hole_ints, exchange_ints, fock_occ, fock_vir, eps_occ, eps_vir):
    high = lax.Precision.HIGHEST
    row = lax.axis_index("row")
    col = lax.axis_index("col")
    t = amplitudes[0]
    packed = pack(t)
    arrived = lax.all_to_all(packed, "col", split_axis=0, concat_axis=0, tiled=True)
    x = arrived.reshape(NO, KT, 128).transpose(1, 0, 2)

    def hop(value, dy, dz, dc):
        return lax.ppermute(value, "row", row_perm(dy, dz, dc))

    v4 = pltpu.with_memory_space_constraint(vvvv.transpose(0, 2, 1, 3), pltpu.HBM)
    k4 = exchange_ints[0].transpose(1, 0, 2)
    bare = hole_ints.reshape(NO * NO, NO * NO)
    fock = jnp.tile(fock_occ, (1, NO))
    pair = jnp.stack([x, hop(x, 1, 0, 0)])
    pair, bare, fock = lax.optimization_barrier((pair, bare, fock))
    ahead = hop(pair, 0, 1, 0)
    behind = hop(pair, 0, 3, 0)
    far = jnp.stack([hop(ahead[0], 0, 1, 0), hop(behind[1], 0, 3, 0)])
    own = jnp.stack([pair, ahead, far, behind])
    other = hop(own, 0, 0, 1)
    own = own.reshape(8, KT, NO, 128)
    other = other.reshape(8, KT, NO, 128)

    rel = jnp.arange(ROWS, dtype=jnp.int32)
    dc, dz, dy = rel // 8, (rel // 2) % 4, rel % 2
    table = ((row // 8 + dy) % 2) * 8 + ((row // 2 + dz) % 4) * 2 + ((row % 2) ^ dc)

    e_row = jnp.arange(EROWS, dtype=jnp.int32)[:, None]
    e_col = jnp.arange(640, dtype=jnp.int32)[None, :]
    want = row * AB + e_row // 4
    cc = e_row % 4
    place = jnp.where(want < 128, cc * 128 + want, 512 + cc * 32 + want - 128)
    onehot = (e_col == place).astype(jnp.bfloat16)

    ghi, glo, chi = prepare(table, own, other, k4)

    def fold(value, flip):
        return value + lax.ppermute(value, "col", [(c, c ^ flip) for c in range(COLS)])

    chi = fold(chi, 1)
    lad = ladder(ghi, glo, v4, (0, 1))
    chi = fold(chi, 2)
    lad = ladder(ghi, glo, v4, (2,), before=lad)
    chi = fold(chi, 4)
    lad = ladder(ghi, glo, v4, (3,), before=lad)
    chi = jnp.stack([chi, hop(chi, 1, 0, 0)])
    lad, block = ladder(ghi, glo, v4, (4,), before=lad, onehot=onehot)
    lad, chi = lax.optimization_barrier((lad, chi))
    scattered = lax.all_to_all(lad, "col", split_axis=0, concat_axis=0, tiled=True)

    chi = jnp.stack([chi] + [hop(chi, 0, dz, 0) for dz in (1, 2, 3)])
    chi = jnp.stack([chi, hop(chi, 0, 0, 1)]).reshape(ROWS, NO, NO * NO)
    sending = post(table, scattered, chi, bare, fock, block)
    back = lax.all_to_all(sending, ("row", "col"), split_axis=0, concat_axis=0, tiled=True)
    back = back.reshape(ROWS, COLS, 2, 2, 256).transpose(2, 3, 1, 0, 4)

    tf = jnp.einsum("jac,cb->jab", t, fock_vir, precision=high)
    tf = tf + jnp.einsum("ac,jcb->jab", fock_vir, t, precision=high)
    first = lax.dynamic_slice_in_dim(eps_occ, row, 1)
    second = lax.dynamic_slice_in_dim(eps_occ, col * 2, 2)
    return finish(first + second, back, tf, eps_vir)[None]


def solution(mesh):
    in_specs = (
        P("row", "col", None, None),
        P("row", None, "col", None),
        P(),
        P("row", None, "col", None),
        P(),
        P(),
        P(),
        P(),
    )
    return jax.shard_map(
        on_device,
        mesh=mesh,
        in_specs=in_specs,
        out_specs=P("row", "col", None, None),
        check_vma=False,
    )
```

```python
import functools

import jax
import jax.numpy as jnp
from jax import lax
from jax.experimental import pallas as pl
from jax.experimental.pallas import tpu as pltpu
from jax.sharding import PartitionSpec as P

NO = 16
NV = 160
ROWS = 16
COLS = 8
AB = NV // ROWS
CB = NV // COLS
KT = 25
VROWS = AB * NV
EROWS = AB * 4
HALF = VROWS // 2
NT = (((1,), (1,)), ((), ()))
VMEM = pl.BlockSpec(memory_space=pltpu.VMEM)


def row_perm(dy, dz, dc):
    def source(r):
        return ((r // 8 + dy) % 2) * 8 + ((r // 2 + dz) % 4) * 2 + ((r % 2) ^ dc)

    return [(source(r), r) for r in range(ROWS)]


def pack_kernel(t_ref, o_ref, tail):
    tail[:, :, 0:32] = t_ref[:, :, 128:NV]
    for c in range(COLS):
        for j in range(2):
            o_ref[c, j, 0:CB, :] = t_ref[j, c * CB : (c + 1) * CB, 0:128]
            tails = [
                tail[j, pl.ds(c * CB + cc, CB // 4, stride=4), :][:, 0:32] for cc in range(4)
            ]
            o_ref[c, j, CB:KT, :] = jnp.concatenate(tails, axis=1)


def pack(t):
    return pl.pallas_call(
        pack_kernel,
        out_shape=jax.ShapeDtypeStruct((COLS, 2, KT, 128), jnp.float32),
        scratch_shapes=[pltpu.VMEM((2, NV, 128), jnp.float32)],
        cost_estimate=pl.CostEstimate(flops=0, bytes_accessed=600000, transcendentals=0),
    )(t)


def split(x):
    hi = x.astype(jnp.bfloat16)
    lo = (x - hi.astype(jnp.float32)).astype(jnp.bfloat16)
    return hi, lo


def convert_block(load, store):
    for kt in range(5):
        if kt < 4:
            x = load(kt, slice(0, 128))
        else:
            x = jnp.concatenate([load(cc, slice(128, NV)) for cc in range(4)], axis=1)
        hi, lo = split(x)
        store(slice(kt * 128, (kt + 1) * 128), hi)
        store(slice(640 + kt * 128, 640 + (kt + 1) * 128), lo)


def split_kernel(group, v_hbm, o_hbm, buf, res, sem_in, sem_out):
    def fetch(a):
        source = v_hbm.at[a, pl.ds(group * 4, 4)]
        return pltpu.make_async_copy(source, buf.at[a], sem_in.at[a])

    def send(a):
        target = o_hbm.at[pl.ds(a * NV, NV)]
        return pltpu.make_async_copy(res.at[pl.ds(a * NV, NV)], target, sem_out.at[a])

    for a in range(AB):
        fetch(a).start()
    for a in range(AB):
        fetch(a).wait()

        def store(lanes, value, a=a):
            res[a * NV : (a + 1) * NV, lanes] = value

        convert_block(lambda cc, lanes, a=a: buf[a, cc, :, lanes], store)
        send(a).start()
    for a in range(AB):
        send(a).wait()


def split_integrals(v, group):
    hbm = pl.BlockSpec(memory_space=pltpu.HBM)
    return pl.pallas_call(
        functools.partial(split_kernel, group),
        out_shape=pltpu.HBM((VROWS, 1280), jnp.bfloat16),
        in_specs=[hbm],
        out_specs=hbm,
        scratch_shapes=[
            pltpu.VMEM((AB, 4, NV, NV), jnp.float32),
            pltpu.VMEM((VROWS, 1280), jnp.bfloat16),
            pltpu.SemaphoreType.DMA((AB,)),
            pltpu.SemaphoreType.DMA((AB,)),
        ],
        compiler_params=pltpu.CompilerParams(vmem_limit_bytes=14 << 20),
        cost_estimate=pl.CostEstimate(flops=0, bytes_accessed=11 << 20, transcendentals=0),
    )(v)


def prepare_kernel(tbl_ref, s_any, q_any, k_any, ghi, glo, chi_ref, s_ref, q_ref, k_ref, sem):
    pairs = ((s_any, s_ref), (q_any, q_ref), (k_any, k_ref))
    copies = [pltpu.make_async_copy(x, y, sem.at[n]) for n, (x, y) in enumerate(pairs)]
    for copy in copies:
        copy.start()
    for rel in range(ROWS):
        if rel % 8 == 0:
            copies[rel // 8].wait()
        ref = s_ref if rel < 8 else q_ref
        start = pl.multiple_of(tbl_ref[rel] * NO, NO)
        for kt in range(KT):
            g, place = (kt // 4, kt % 4) if kt < CB else (kt - CB, 4)
            hi, lo = split(ref[rel % 8, kt])
            ghi[g, pl.ds(start, NO), place * 128 : (place + 1) * 128] = hi
            ghi[g, pl.ds(start, NO), 640 + place * 128 : 640 + (place + 1) * 128] = hi
            glo[g, pl.ds(start, NO), place * 128 : (place + 1) * 128] = lo
    copies[2].wait()
    chi = jnp.zeros((NO * NO, NO), jnp.float32)
    for g in range(5):
        parts = [k_ref[g * 4 + cc, :, 0:128] for cc in range(4)]
        parts.append(
            jnp.concatenate([k_ref[g * 4 + cc, :, 128:NV] for cc in range(4)], axis=1)
        )
        hi, lo = split(jnp.concatenate(parts, axis=1))
        chi = chi + dot_nt(ghi[g, :, 0:640], hi) + dot_nt(ghi[g, :, 0:640], lo)
        chi = chi + dot_nt(glo[g], hi)
    chi_ref[...] = chi.T


def dot_nt(x, y):
    return lax.dot_general(x, y, NT, preferred_element_type=jnp.float32)


def prepare(tbl, s, q, k):
    return pl.pallas_call(
        prepare_kernel,
        out_shape=(
            pltpu.VMEM((5, NO * NO, 1280), jnp.bfloat16),
            pltpu.VMEM((5, NO * NO, 640), jnp.bfloat16),
            jax.ShapeDtypeStruct((NO, NO * NO), jnp.float32),
        ),
        in_specs=[pl.BlockSpec(memory_space=pltpu.SMEM)]
        + [pl.BlockSpec(memory_space=pltpu.HBM)] * 3,
        out_specs=(VMEM, VMEM, VMEM),
        scratch_shapes=[
            pltpu.VMEM((8, KT, NO, 128), jnp.float32),
            pltpu.VMEM((8, KT, NO, 128), jnp.float32),
            pltpu.VMEM((CB, NO, NV), jnp.float32),
            pltpu.SemaphoreType.DMA((3,)),
        ],
        compiler_params=pltpu.CompilerParams(vmem_limit_bytes=11 << 20),
        cost_estimate=pl.CostEstimate(flops=0, bytes_accessed=8 << 20, transcendentals=0),
    )(tbl, s, q, k)


def ladder_kernel(group, fresh, last, ghi, glo, *refs):
    refs = list(refs)
    v_hbm = refs.pop(0) if fresh else None
    ready = None if fresh else refs.pop(0)
    before = None if fresh else refs.pop(0)
    out = refs.pop(0)
    if fresh:
        buf, parts, sem = refs
        copies = []
        for n in range(2):
            source = v_hbm.at[pl.ds(n * (AB // 2), AB // 2), pl.ds(0, 4)]
            copies.append(pltpu.make_async_copy(source, buf.at[n], sem.at[n]))
            copies[-1].start()
        for n in range(2):
            copies[n].wait()
            for a in range(AB // 2):

                def store(lanes, value, n=n, a=a):
                    parts[n, a * NV : (a + 1) * NV, lanes] = value

                convert_block(lambda cc, lanes, n=n, a=a: buf[n, a, cc, :, lanes], store)
            part = dot_nt(parts[n], ghi[0]) + dot_nt(parts[n, :, 0:640], glo[0])
            out[n * HALF : (n + 1) * HALF, :] = part
        return
    total = before[...] + dot_nt(ready[...], ghi[group])
    total = total + dot_nt(ready[:, 0:640], glo[group])
    if not last:
        out[...] = total
        return
    for a in range(AB):
        for c in range(COLS):
            start = a * NV + c * CB
            out[c, a * CB : (a + 1) * CB, :] = total[start : start + CB, :]


def ladder(ghi, glo, source, group, before=None):
    fresh, last = before is None, group == 4
    operands = [ghi, glo, source]
    in_specs = [VMEM, VMEM, pl.BlockSpec(memory_space=pltpu.HBM) if fresh else VMEM]
    if not fresh:
        operands.append(before)
        in_specs.append(VMEM)
    scratch = []
    if fresh:
        scratch = [
            pltpu.VMEM((2, AB // 2, 4, NV, NV), jnp.float32),
            pltpu.VMEM((2, HALF, 1280), jnp.bfloat16),
            pltpu.SemaphoreType.DMA((2,)),
        ]
    if last:
        out_shape = pltpu.HBM((COLS, AB * CB, NO * NO), jnp.float32)
        out_specs = pl.BlockSpec((COLS, AB * CB, NO * NO), lambda: (0, 0, 0))
    else:
        out_shape = pltpu.VMEM((VROWS, NO * NO), jnp.float32)
        out_specs = VMEM
    return pl.pallas_call(
        functools.partial(ladder_kernel, group, fresh, last),
        out_shape=out_shape,
        in_specs=in_specs,
        out_specs=out_specs,
        scratch_shapes=scratch,
        compiler_params=pltpu.CompilerParams(vmem_limit_bytes=(14 if fresh else 11) << 20),
        cost_estimate=pl.CostEstimate(
            flops=3 * 2 * 1600 * 640 * 256,
            bytes_accessed=8 << 20,
            transcendentals=0,
        ),
    )(*operands)


def block_kernel(ghi, glo, e_ref, p_ref):
    for g in range(5):
        block = dot_nt(e_ref[...], ghi[g, :, 0:640]) + dot_nt(e_ref[...], glo[g])
        for a in range(AB):
            row = a * CB + g * 4
            p_ref[row : row + 4, :] = block[a * 4 : a * 4 + 4, :]


def own_block(ghi, glo, onehot):
    return pl.pallas_call(
        block_kernel,
        out_shape=jax.ShapeDtypeStruct((AB * CB, NO * NO), jnp.float32),
        in_specs=[VMEM] * 3,
        out_specs=VMEM,
        compiler_params=pltpu.CompilerParams(vmem_limit_bytes=4 << 20),
        cost_estimate=pl.CostEstimate(flops=1 << 31, bytes_accessed=6 << 20, transcendentals=0),
    )(ghi, glo, onehot)


def post_kernel(tbl_ref, x_ref, chi_ref, w_ref, f_ref, p_ref, o_ref, c0, c1, r0, r1, m1):
    owner = lax.broadcasted_iota(jnp.int32, (NO, NO * NO), 1) // NO
    for rel in range(ROWS):
        k = tbl_ref[rel]
        piece = chi_ref[rel] + w_ref[pl.ds(pl.multiple_of(k * NO, NO), NO), :]
        piece = piece - jnp.where(owner == k, f_ref[...], 0.0)
        c0[pl.ds(k, NO, stride=NO), :] = piece[:, 0:128]
        c1[pl.ds(k, NO, stride=NO), :] = piece[:, 128:256]
    chi = jnp.concatenate([c0[...], c1[...]], axis=1)
    total = x_ref[0]
    for c in range(1, COLS):
        total = total + x_ref[c]
    total = total + jnp.dot(
        p_ref[...], chi, precision=lax.Precision.HIGHEST, preferred_element_type=jnp.float32
    )
    total = jnp.concatenate([total, jnp.zeros((256 - AB * CB, NO * NO), jnp.float32)], axis=0)
    raw = total.T
    r0[...] = raw[:, 0:128]
    r1[...] = raw[:, 128:256]
    for i in range(NO):
        m1[i * NO : (i + 1) * NO, 0:128] = r0[pl.ds(i, NO, stride=NO), :]
        m1[i * NO : (i + 1) * NO, 128:256] = r1[pl.ds(i, NO, stride=NO), :]
    flipped = m1[...]
    for d in range(ROWS * COLS):
        o_ref[d, 0:2, :] = raw[2 * d : 2 * d + 2, :]
        o_ref[d, 2:4, :] = flipped[2 * d : 2 * d + 2, :]


def post(tbl, scattered, chi, bare, fock, block):
    return pl.pallas_call(
        post_kernel,
        out_shape=jax.ShapeDtypeStruct((ROWS * COLS, 4, 256), jnp.float32),
        in_specs=[pl.BlockSpec(memory_space=pltpu.SMEM)] + [VMEM] * 5,
        out_specs=VMEM,
        scratch_shapes=[pltpu.VMEM((NO * NO, 128), jnp.float32)] * 4
        + [pltpu.VMEM((NO * NO, 256), jnp.float32)],
        compiler_params=pltpu.CompilerParams(vmem_limit_bytes=12 << 20),
        cost_estimate=pl.CostEstimate(
            flops=6 * 2 * 200 * 65536, bytes_accessed=3 << 20, transcendentals=0
        ),
    )(tbl, scattered, chi, bare, fock, block)


def final_kernel(e_ref, x_ref, tf_ref, vrow_ref, vcol_ref, o_ref, left, right):
    for o in range(2):
        for s in range(2):
            for a in range(AB):
                pieces = [x_ref[o, s, c, :, a * CB : (a + 1) * CB] for c in range(COLS)]
                line = jnp.concatenate(pieces, axis=1)
                left[o, s, pl.ds(a, ROWS, stride=AB), :] = line[:, 0:128]
                right[o, s, pl.ds(a, ROWS, stride=AB), 0:32] = line[:, 128:NV]
    for s in range(2):
        full = [
            jnp.concatenate([left[o, s], right[o, s, :, 0:32]], axis=1) for o in range(2)
        ]
        total = full[0] + full[1].T + tf_ref[s]
        den = (e_ref[s] - vcol_ref[...]) - vrow_ref[...]
        o_ref[s] = total / den


def finish(e, x, tf, eps_vir):
    return pl.pallas_call(
        final_kernel,
        out_shape=jax.ShapeDtypeStruct((2, NV, NV), jnp.float32),
        in_specs=[pl.BlockSpec(memory_space=pltpu.SMEM)]
        + [pl.BlockSpec(memory_space=pltpu.VMEM)] * 4,
        out_specs=pl.BlockSpec(memory_space=pltpu.VMEM),
        scratch_shapes=[pltpu.VMEM((2, 2, NV, 128), jnp.float32)] * 2,
        cost_estimate=pl.CostEstimate(flops=0, bytes_accessed=2 << 20, transcendentals=0),
    )(e, x, tf, eps_vir.reshape(1, NV), eps_vir.reshape(NV, 1))


def on_device(amplitudes, vvvv, hole_ints, exchange_ints, fock_occ, fock_vir, eps_occ, eps_vir):
    high = lax.Precision.HIGHEST
    row = lax.axis_index("row")
    col = lax.axis_index("col")
    t = amplitudes[0]
    packed = pack(t)
    arrived = lax.all_to_all(packed, "col", split_axis=0, concat_axis=0, tiled=True)
    x = arrived.reshape(NO, KT, 128).transpose(1, 0, 2)

    def hop(value, dy, dz, dc):
        return lax.ppermute(value, "row", row_perm(dy, dz, dc))

    v4 = pltpu.with_memory_space_constraint(vvvv.transpose(0, 2, 1, 3), pltpu.HBM)
    k4 = exchange_ints[0].transpose(1, 0, 2)
    pair = jnp.stack([x, hop(x, 1, 0, 0)])
    pair, opening = lax.optimization_barrier((pair, split_integrals(v4, 1)))
    ahead = hop(pair, 0, 1, 0)
    behind = hop(pair, 0, 3, 0)
    second, third = split_integrals(v4, 2), split_integrals(v4, 3)
    ahead, behind, second, third = lax.optimization_barrier((ahead, behind, second, third))
    far = jnp.stack([hop(ahead[0], 0, 1, 0), hop(behind[1], 0, 3, 0)])
    own = jnp.stack([pair, ahead, far, behind])
    other = hop(own, 0, 0, 1)
    fourth = split_integrals(v4, 4)
    own = own.reshape(8, KT, NO, 128)
    other = other.reshape(8, KT, NO, 128)

    rel = jnp.arange(ROWS, dtype=jnp.int32)
    dc, dz, dy = rel // 8, (rel // 2) % 4, rel % 2
    table = ((row // 8 + dy) % 2) * 8 + ((row // 2 + dz) % 4) * 2 + ((row % 2) ^ dc)

    e_row = jnp.arange(EROWS, dtype=jnp.int32)[:, None]
    e_col = jnp.arange(640, dtype=jnp.int32)[None, :]
    want = row * AB + e_row // 4
    cc = e_row % 4
    place = jnp.where(want < 128, cc * 128 + want, 512 + cc * 32 + want - 128)
    onehot = (e_col == place).astype(jnp.bfloat16)

    hbm = lambda value: pltpu.with_memory_space_constraint(value, pltpu.HBM)
    ghi, glo, chi = prepare(table, hbm(own), hbm(other), hbm(k4))

    def fold(value, flip):
        return value + lax.ppermute(value, "col", [(c, c ^ flip) for c in range(COLS)])

    chi = fold(chi, 1)
    lad = ladder(ghi, glo, v4, 0)
    chi = fold(chi, 2)
    lad = ladder(ghi, glo, opening, 1, before=lad)
    lad = ladder(ghi, glo, second, 2, before=lad)
    chi = fold(chi, 4)
    lad = ladder(ghi, glo, third, 3, before=lad)
    chi = jnp.stack([chi, hop(chi, 1, 0, 0)])
    lad = ladder(ghi, glo, fourth, 4, before=lad)
    lad, chi, holes = lax.optimization_barrier((lad, chi, hole_ints))
    scattered = lax.all_to_all(lad, "col", split_axis=0, concat_axis=0, tiled=True)

    chi = jnp.stack([chi] + [hop(chi, 0, dz, 0) for dz in (1, 2, 3)])
    chi = jnp.stack([chi, hop(chi, 0, 0, 1)]).reshape(ROWS, NO, NO * NO)
    block = own_block(ghi, glo, onehot)
    bare = holes.reshape(NO * NO, NO * NO)
    fock = jnp.tile(fock_occ, (1, NO))
    sending = post(table, scattered, chi, bare, fock, block)
    back = lax.all_to_all(sending, ("row", "col"), split_axis=0, concat_axis=0, tiled=True)
    back = back.reshape(ROWS, COLS, 2, 2, 256).transpose(2, 3, 1, 0, 4)

    tf = jnp.einsum("jac,cb->jab", t, fock_vir, precision=high)
    tf = tf + jnp.einsum("ac,jcb->jab", fock_vir, t, precision=high)
    first = lax.dynamic_slice_in_dim(eps_occ, row, 1)
    second = lax.dynamic_slice_in_dim(eps_occ, col * 2, 2)
    return finish(first + second, back, tf, eps_vir)[None]


def solution(mesh):
    in_specs = (
        P("row", "col", None, None),
        P("row", None, "col", None),
        P(),
        P("row", None, "col", None),
        P(),
        P(),
        P(),
        P(),
    )
    return jax.shard_map(
        on_device,
        mesh=mesh,
        in_specs=in_specs,
        out_specs=P("row", "col", None, None),
        check_vma=False,
    )
```

```python
import functools

import jax
import jax.numpy as jnp
from jax import lax
from jax.experimental import pallas as pl
from jax.experimental.pallas import tpu as pltpu
from jax.sharding import PartitionSpec as P

NO = 16
NV = 160
ROWS = 16
COLS = 8
AB = NV // ROWS
CB = NV // COLS
KT = 25
VROWS = AB * NV
EROWS = AB * 4
HALF = VROWS // 2
NT = (((1,), (1,)), ((), ()))
VMEM = pl.BlockSpec(memory_space=pltpu.VMEM)


def row_perm(dy, dz, dc):
    def source(r):
        return ((r // 8 + dy) % 2) * 8 + ((r // 2 + dz) % 4) * 2 + ((r % 2) ^ dc)

    return [(source(r), r) for r in range(ROWS)]


def pack_kernel(t_ref, o_ref, tail):
    tail[:, :, 0:32] = t_ref[:, :, 128:NV]
    for c in range(COLS):
        for j in range(2):
            o_ref[c, j, 0:CB, :] = t_ref[j, c * CB : (c + 1) * CB, 0:128]
            tails = [
                tail[j, pl.ds(c * CB + cc, CB // 4, stride=4), :][:, 0:32] for cc in range(4)
            ]
            o_ref[c, j, CB:KT, :] = jnp.concatenate(tails, axis=1)


def pack(t):
    return pl.pallas_call(
        pack_kernel,
        out_shape=jax.ShapeDtypeStruct((COLS, 2, KT, 128), jnp.float32),
        scratch_shapes=[pltpu.VMEM((2, NV, 128), jnp.float32)],
        cost_estimate=pl.CostEstimate(flops=0, bytes_accessed=600000, transcendentals=0),
    )(t)


def split(x):
    hi = x.astype(jnp.bfloat16)
    lo = (x - hi.astype(jnp.float32)).astype(jnp.bfloat16)
    return hi, lo


def convert_block(load, store):
    for kt in range(5):
        if kt < 4:
            x = load(kt, slice(0, 128))
        else:
            x = jnp.concatenate([load(cc, slice(128, NV)) for cc in range(4)], axis=1)
        hi, lo = split(x)
        store(slice(kt * 128, (kt + 1) * 128), hi)
        store(slice(640 + kt * 128, 640 + (kt + 1) * 128), lo)


def split_kernel(group, v_hbm, o_hbm, buf, res, sem_in, sem_out):
    def fetch(a):
        source = v_hbm.at[a, pl.ds(group * 4, 4)]
        return pltpu.make_async_copy(source, buf.at[a], sem_in.at[a])

    def send(a):
        target = o_hbm.at[pl.ds(a * NV, NV)]
        return pltpu.make_async_copy(res.at[pl.ds(a * NV, NV)], target, sem_out.at[a])

    for a in range(AB):
        fetch(a).start()
    for a in range(AB):
        fetch(a).wait()

        def store(lanes, value, a=a):
            res[a * NV : (a + 1) * NV, lanes] = value

        convert_block(lambda cc, lanes, a=a: buf[a, cc, :, lanes], store)
        send(a).start()
    for a in range(AB):
        send(a).wait()


def split_integrals(v, group):
    hbm = pl.BlockSpec(memory_space=pltpu.HBM)
    return pl.pallas_call(
        functools.partial(split_kernel, group),
        out_shape=pltpu.HBM((VROWS, 1280), jnp.bfloat16),
        in_specs=[hbm],
        out_specs=hbm,
        scratch_shapes=[
            pltpu.VMEM((AB, 4, NV, NV), jnp.float32),
            pltpu.VMEM((VROWS, 1280), jnp.bfloat16),
            pltpu.SemaphoreType.DMA((AB,)),
            pltpu.SemaphoreType.DMA((AB,)),
        ],
        compiler_params=pltpu.CompilerParams(vmem_limit_bytes=14 << 20),
        cost_estimate=pl.CostEstimate(flops=0, bytes_accessed=11 << 20, transcendentals=0),
    )(v)


def prepare_kernel(tbl_ref, s_any, q_any, k_any, ghi, glo, chi_ref, s_ref, q_ref, k_ref, sem):
    pairs = ((s_any, s_ref), (q_any, q_ref), (k_any, k_ref))
    copies = [pltpu.make_async_copy(x, y, sem.at[n]) for n, (x, y) in enumerate(pairs)]
    for copy in copies:
        copy.start()
    for rel in range(ROWS):
        if rel % 8 == 0:
            copies[rel // 8].wait()
        ref = s_ref if rel < 8 else q_ref
        start = pl.multiple_of(tbl_ref[rel] * NO, NO)
        for kt in range(KT):
            g, place = (kt // 4, kt % 4) if kt < CB else (kt - CB, 4)
            hi, lo = split(ref[rel % 8, kt])
            ghi[g, pl.ds(start, NO), place * 128 : (place + 1) * 128] = hi
            ghi[g, pl.ds(start, NO), 640 + place * 128 : 640 + (place + 1) * 128] = hi
            glo[g, pl.ds(start, NO), place * 128 : (place + 1) * 128] = lo
    copies[2].wait()
    chi = jnp.zeros((NO * NO, NO), jnp.float32)
    for g in range(5):
        parts = [k_ref[g * 4 + cc, :, 0:128] for cc in range(4)]
        parts.append(
            jnp.concatenate([k_ref[g * 4 + cc, :, 128:NV] for cc in range(4)], axis=1)
        )
        hi, lo = split(jnp.concatenate(parts, axis=1))
        chi = chi + dot_nt(ghi[g, :, 0:640], hi) + dot_nt(ghi[g, :, 0:640], lo)
        chi = chi + dot_nt(glo[g], hi)
    chi_ref[...] = chi.T


def dot_nt(x, y):
    return lax.dot_general(x, y, NT, preferred_element_type=jnp.float32)


def prepare(tbl, s, q, k):
    return pl.pallas_call(
        prepare_kernel,
        out_shape=(
            pltpu.VMEM((5, NO * NO, 1280), jnp.bfloat16),
            pltpu.VMEM((5, NO * NO, 640), jnp.bfloat16),
            jax.ShapeDtypeStruct((NO, NO * NO), jnp.float32),
        ),
        in_specs=[pl.BlockSpec(memory_space=pltpu.SMEM)]
        + [pl.BlockSpec(memory_space=pltpu.HBM)] * 3,
        out_specs=(VMEM, VMEM, VMEM),
        scratch_shapes=[
            pltpu.VMEM((8, KT, NO, 128), jnp.float32),
            pltpu.VMEM((8, KT, NO, 128), jnp.float32),
            pltpu.VMEM((CB, NO, NV), jnp.float32),
            pltpu.SemaphoreType.DMA((3,)),
        ],
        compiler_params=pltpu.CompilerParams(vmem_limit_bytes=11 << 20),
        cost_estimate=pl.CostEstimate(flops=0, bytes_accessed=8 << 20, transcendentals=0),
    )(tbl, s, q, k)


def ladder_kernel(group, fresh, last, ghi, glo, *refs):
    refs = list(refs)
    v_hbm = refs.pop(0) if fresh else None
    ready = None if fresh else refs.pop(0)
    before = None if fresh else refs.pop(0)
    out = refs.pop(0)
    if fresh:
        buf, parts, sem = refs
        copies = []
        for n in range(2):
            source = v_hbm.at[pl.ds(n * (AB // 2), AB // 2), pl.ds(0, 4)]
            copies.append(pltpu.make_async_copy(source, buf.at[n], sem.at[n]))
            copies[-1].start()
        for n in range(2):
            copies[n].wait()
            for a in range(AB // 2):

                def store(lanes, value, n=n, a=a):
                    parts[n, a * NV : (a + 1) * NV, lanes] = value

                convert_block(lambda cc, lanes, n=n, a=a: buf[n, a, cc, :, lanes], store)
            part = dot_nt(parts[n], ghi[0]) + dot_nt(parts[n, :, 0:640], glo[0])
            out[n * HALF : (n + 1) * HALF, :] = part
        return
    total = before[...] + dot_nt(ready[...], ghi[group])
    total = total + dot_nt(ready[:, 0:640], glo[group])
    if not last:
        out[...] = total
        return
    for a in range(AB):
        for c in range(COLS):
            start = a * NV + c * CB
            out[c, a * CB : (a + 1) * CB, :] = total[start : start + CB, :]


def ladder(ghi, glo, source, group, before=None):
    fresh, last = before is None, group == 4
    operands = [ghi, glo, source]
    in_specs = [VMEM, VMEM, pl.BlockSpec(memory_space=pltpu.HBM) if fresh else VMEM]
    if not fresh:
        operands.append(before)
        in_specs.append(VMEM)
    scratch = []
    if fresh:
        scratch = [
            pltpu.VMEM((2, AB // 2, 4, NV, NV), jnp.float32),
            pltpu.VMEM((2, HALF, 1280), jnp.bfloat16),
            pltpu.SemaphoreType.DMA((2,)),
        ]
    if last:
        out_shape = pltpu.HBM((COLS, AB * CB, NO * NO), jnp.float32)
        out_specs = pl.BlockSpec((COLS, AB * CB, NO * NO), lambda: (0, 0, 0))
    else:
        out_shape = pltpu.VMEM((VROWS, NO * NO), jnp.float32)
        out_specs = VMEM
    return pl.pallas_call(
        functools.partial(ladder_kernel, group, fresh, last),
        out_shape=out_shape,
        in_specs=in_specs,
        out_specs=out_specs,
        scratch_shapes=scratch,
        compiler_params=pltpu.CompilerParams(vmem_limit_bytes=(14 if fresh else 11) << 20),
        cost_estimate=pl.CostEstimate(
            flops=3 * 2 * 1600 * 640 * 256,
            bytes_accessed=8 << 20,
            transcendentals=0,
        ),
    )(*operands)


def block_kernel(ghi, glo, e_ref, p_ref):
    for g in range(5):
        block = dot_nt(e_ref[...], ghi[g, :, 0:640]) + dot_nt(e_ref[...], glo[g])
        for a in range(AB):
            row = a * CB + g * 4
            p_ref[row : row + 4, :] = block[a * 4 : a * 4 + 4, :]


def own_block(ghi, glo, onehot):
    return pl.pallas_call(
        block_kernel,
        out_shape=jax.ShapeDtypeStruct((AB * CB, NO * NO), jnp.float32),
        in_specs=[VMEM] * 3,
        out_specs=VMEM,
        compiler_params=pltpu.CompilerParams(vmem_limit_bytes=4 << 20),
        cost_estimate=pl.CostEstimate(flops=1 << 31, bytes_accessed=6 << 20, transcendentals=0),
    )(ghi, glo, onehot)


def post_kernel(tbl_ref, x_ref, chi_ref, w_ref, f_ref, p_ref, o_ref, c0, c1, r0, r1, m1):
    owner = lax.broadcasted_iota(jnp.int32, (NO, NO * NO), 1) // NO
    for rel in range(ROWS):
        k = tbl_ref[rel]
        piece = chi_ref[rel] + w_ref[pl.ds(pl.multiple_of(k * NO, NO), NO), :]
        piece = piece - jnp.where(owner == k, f_ref[...], 0.0)
        c0[pl.ds(k, NO, stride=NO), :] = piece[:, 0:128]
        c1[pl.ds(k, NO, stride=NO), :] = piece[:, 128:256]
    chi = jnp.concatenate([c0[...], c1[...]], axis=1)
    total = x_ref[0]
    for c in range(1, COLS):
        total = total + x_ref[c]
    total = total + jnp.dot(
        p_ref[...], chi, precision=lax.Precision.HIGHEST, preferred_element_type=jnp.float32
    )
    total = jnp.concatenate([total, jnp.zeros((256 - AB * CB, NO * NO), jnp.float32)], axis=0)
    raw = total.T
    r0[...] = raw[:, 0:128]
    r1[...] = raw[:, 128:256]
    for i in range(NO):
        m1[i * NO : (i + 1) * NO, 0:128] = r0[pl.ds(i, NO, stride=NO), :]
        m1[i * NO : (i + 1) * NO, 128:256] = r1[pl.ds(i, NO, stride=NO), :]
    flipped = m1[...]
    for d in range(ROWS * COLS):
        o_ref[d, 0:2, :] = raw[2 * d : 2 * d + 2, :]
        o_ref[d, 2:4, :] = flipped[2 * d : 2 * d + 2, :]


def post(tbl, scattered, chi, bare, fock, block):
    return pl.pallas_call(
        post_kernel,
        out_shape=jax.ShapeDtypeStruct((ROWS * COLS, 4, 256), jnp.float32),
        in_specs=[pl.BlockSpec(memory_space=pltpu.SMEM)] + [VMEM] * 5,
        out_specs=VMEM,
        scratch_shapes=[pltpu.VMEM((NO * NO, 128), jnp.float32)] * 4
        + [pltpu.VMEM((NO * NO, 256), jnp.float32)],
        compiler_params=pltpu.CompilerParams(vmem_limit_bytes=12 << 20),
        cost_estimate=pl.CostEstimate(
            flops=6 * 2 * 200 * 65536, bytes_accessed=3 << 20, transcendentals=0
        ),
    )(tbl, scattered, chi, bare, fock, block)


def final_kernel(e_ref, x_ref, tf_ref, vrow_ref, vcol_ref, o_ref, left, right):
    for o in range(2):
        for s in range(2):
            for a in range(AB):
                pieces = [x_ref[o, s, c, :, a * CB : (a + 1) * CB] for c in range(COLS)]
                line = jnp.concatenate(pieces, axis=1)
                left[o, s, pl.ds(a, ROWS, stride=AB), :] = line[:, 0:128]
                right[o, s, pl.ds(a, ROWS, stride=AB), 0:32] = line[:, 128:NV]
    for s in range(2):
        full = [
            jnp.concatenate([left[o, s], right[o, s, :, 0:32]], axis=1) for o in range(2)
        ]
        total = full[0] + full[1].T + tf_ref[s]
        den = (e_ref[s] - vcol_ref[...]) - vrow_ref[...]
        o_ref[s] = total / den


def finish(e, x, tf, eps_vir):
    return pl.pallas_call(
        final_kernel,
        out_shape=jax.ShapeDtypeStruct((2, NV, NV), jnp.float32),
        in_specs=[pl.BlockSpec(memory_space=pltpu.SMEM)]
        + [pl.BlockSpec(memory_space=pltpu.VMEM)] * 4,
        out_specs=pl.BlockSpec(memory_space=pltpu.VMEM),
        scratch_shapes=[pltpu.VMEM((2, 2, NV, 128), jnp.float32)] * 2,
        cost_estimate=pl.CostEstimate(flops=0, bytes_accessed=2 << 20, transcendentals=0),
    )(e, x, tf, eps_vir.reshape(1, NV), eps_vir.reshape(NV, 1))


def on_device(amplitudes, vvvv, hole_ints, exchange_ints, fock_occ, fock_vir, eps_occ, eps_vir):
    high = lax.Precision.HIGHEST
    row = lax.axis_index("row")
    col = lax.axis_index("col")
    t = amplitudes[0]
    packed = pack(t)
    arrived = lax.all_to_all(packed, "col", split_axis=0, concat_axis=0, tiled=True)
    x = arrived.reshape(NO, KT, 128).transpose(1, 0, 2)

    def hop(value, dy, dz, dc):
        return lax.ppermute(value, "row", row_perm(dy, dz, dc))

    v4 = pltpu.with_memory_space_constraint(vvvv.transpose(0, 2, 1, 3), pltpu.HBM)
    k4 = exchange_ints[0].transpose(1, 0, 2)
    pair = jnp.stack([x, hop(x, 1, 0, 0)])
    pair, opening = lax.optimization_barrier((pair, split_integrals(v4, 1)))
    ahead = hop(pair, 0, 1, 0)
    behind = hop(pair, 0, 3, 0)
    ahead, behind, second = lax.optimization_barrier((ahead, behind, split_integrals(v4, 2)))
    far = [hop(ahead[0], 0, 1, 0), hop(behind[1], 0, 3, 0)]
    far, third = lax.optimization_barrier((far, split_integrals(v4, 3)))
    far = jnp.stack(far)
    own = jnp.stack([pair, ahead, far, behind])
    other = hop(own, 0, 0, 1)
    fourth = split_integrals(v4, 4)
    own = own.reshape(8, KT, NO, 128)
    other = other.reshape(8, KT, NO, 128)

    rel = jnp.arange(ROWS, dtype=jnp.int32)
    dc, dz, dy = rel // 8, (rel // 2) % 4, rel % 2
    table = ((row // 8 + dy) % 2) * 8 + ((row // 2 + dz) % 4) * 2 + ((row % 2) ^ dc)

    e_row = jnp.arange(EROWS, dtype=jnp.int32)[:, None]
    e_col = jnp.arange(640, dtype=jnp.int32)[None, :]
    want = row * AB + e_row // 4
    cc = e_row % 4
    place = jnp.where(want < 128, cc * 128 + want, 512 + cc * 32 + want - 128)
    onehot = (e_col == place).astype(jnp.bfloat16)

    hbm = lambda value: pltpu.with_memory_space_constraint(value, pltpu.HBM)
    ghi, glo, chi = prepare(table, hbm(own), hbm(other), hbm(k4))

    def fold(value, flip):
        return value + lax.ppermute(value, "col", [(c, c ^ flip) for c in range(COLS)])

    chi = fold(chi, 1)
    lad = ladder(ghi, glo, v4, 0)
    chi = fold(chi, 2)
    lad = ladder(ghi, glo, opening, 1, before=lad)
    lad = ladder(ghi, glo, second, 2, before=lad)
    chi = fold(chi, 4)
    lad = ladder(ghi, glo, third, 3, before=lad)
    chi = jnp.stack([chi, hop(chi, 1, 0, 0)])
    lad = ladder(ghi, glo, fourth, 4, before=lad)
    lad, chi, holes = lax.optimization_barrier((lad, chi, hole_ints))
    scattered = lax.all_to_all(lad, "col", split_axis=0, concat_axis=0, tiled=True)

    chi = jnp.stack([chi] + [hop(chi, 0, dz, 0) for dz in (1, 2, 3)])
    chi = jnp.stack([chi, hop(chi, 0, 0, 1)]).reshape(ROWS, NO, NO * NO)
    block = own_block(ghi, glo, onehot)
    bare = holes.reshape(NO * NO, NO * NO)
    fock = jnp.tile(fock_occ, (1, NO))
    sending = post(table, scattered, chi, bare, fock, block)
    back = lax.all_to_all(sending, ("row", "col"), split_axis=0, concat_axis=0, tiled=True)
    back = back.reshape(ROWS, COLS, 2, 2, 256).transpose(2, 3, 1, 0, 4)

    tf = jnp.einsum("jac,cb->jab", t, fock_vir, precision=high)
    tf = tf + jnp.einsum("ac,jcb->jab", fock_vir, t, precision=high)
    first = lax.dynamic_slice_in_dim(eps_occ, row, 1)
    second = lax.dynamic_slice_in_dim(eps_occ, col * 2, 2)
    return finish(first + second, back, tf, eps_vir)[None]


def solution(mesh):
    in_specs = (
        P("row", "col", None, None),
        P("row", None, "col", None),
        P(),
        P("row", None, "col", None),
        P(),
        P(),
        P(),
        P(),
    )
    return jax.shard_map(
        on_device,
        mesh=mesh,
        in_specs=in_specs,
        out_specs=P("row", "col", None, None),
        check_vma=False,
    )
```

```python
import functools

import jax
import jax.numpy as jnp
from jax import lax
from jax.experimental import pallas as pl
from jax.experimental.pallas import tpu as pltpu
from jax.sharding import PartitionSpec as P

NO = 16
NV = 160
ROWS = 16
COLS = 8
AB = NV // ROWS
CB = NV // COLS
KT = 25
VROWS = AB * NV
EROWS = AB * 4
HALF = VROWS // 2
NT = (((1,), (1,)), ((), ()))
VMEM = pl.BlockSpec(memory_space=pltpu.VMEM)


def row_perm(dy, dz, dc):
    def source(r):
        return ((r // 8 + dy) % 2) * 8 + ((r // 2 + dz) % 4) * 2 + ((r % 2) ^ dc)

    return [(source(r), r) for r in range(ROWS)]


def pack_kernel(t_ref, o_ref, tail):
    tail[:, :, 0:32] = t_ref[:, :, 128:NV]
    for c in range(COLS):
        for j in range(2):
            o_ref[c, j, 0:CB, :] = t_ref[j, c * CB : (c + 1) * CB, 0:128]
            tails = [
                tail[j, pl.ds(c * CB + cc, CB // 4, stride=4), :][:, 0:32] for cc in range(4)
            ]
            o_ref[c, j, CB:KT, :] = jnp.concatenate(tails, axis=1)


def pack(t):
    return pl.pallas_call(
        pack_kernel,
        out_shape=jax.ShapeDtypeStruct((COLS, 2, KT, 128), jnp.float32),
        scratch_shapes=[pltpu.VMEM((2, NV, 128), jnp.float32)],
        cost_estimate=pl.CostEstimate(flops=0, bytes_accessed=600000, transcendentals=0),
    )(t)


def split(x):
    hi = x.astype(jnp.bfloat16)
    lo = (x - hi.astype(jnp.float32)).astype(jnp.bfloat16)
    return hi, lo


def convert_block(load, store):
    for kt in range(5):
        if kt < 4:
            x = load(kt, slice(0, 128))
        else:
            x = jnp.concatenate([load(cc, slice(128, NV)) for cc in range(4)], axis=1)
        hi, lo = split(x)
        store(slice(kt * 128, (kt + 1) * 128), hi)
        store(slice(640 + kt * 128, 640 + (kt + 1) * 128), lo)


def split_kernel(group, v_hbm, o_hbm, buf, res, sem_in, sem_out):
    def fetch(a):
        source = v_hbm.at[a, pl.ds(group * 4, 4)]
        return pltpu.make_async_copy(source, buf.at[a], sem_in.at[a])

    def send(a):
        target = o_hbm.at[pl.ds(a * NV, NV)]
        return pltpu.make_async_copy(res.at[pl.ds(a * NV, NV)], target, sem_out.at[a])

    for a in range(AB):
        fetch(a).start()
    for a in range(AB):
        fetch(a).wait()

        def store(lanes, value, a=a):
            res[a * NV : (a + 1) * NV, lanes] = value

        convert_block(lambda cc, lanes, a=a: buf[a, cc, :, lanes], store)
        send(a).start()
    for a in range(AB):
        send(a).wait()


def split_integrals(v, group):
    hbm = pl.BlockSpec(memory_space=pltpu.HBM)
    return pl.pallas_call(
        functools.partial(split_kernel, group),
        out_shape=pltpu.HBM((VROWS, 1280), jnp.bfloat16),
        in_specs=[hbm],
        out_specs=hbm,
        scratch_shapes=[
            pltpu.VMEM((AB, 4, NV, NV), jnp.float32),
            pltpu.VMEM((VROWS, 1280), jnp.bfloat16),
            pltpu.SemaphoreType.DMA((AB,)),
            pltpu.SemaphoreType.DMA((AB,)),
        ],
        compiler_params=pltpu.CompilerParams(vmem_limit_bytes=14 << 20),
        cost_estimate=pl.CostEstimate(flops=0, bytes_accessed=11 << 20, transcendentals=0),
    )(v)


def prepare_kernel(tbl_ref, s_any, q_any, k_any, ghi, glo, chi_ref, s_ref, q_ref, k_ref, sem):
    pairs = ((s_any, s_ref), (q_any, q_ref), (k_any, k_ref))
    copies = [pltpu.make_async_copy(x, y, sem.at[n]) for n, (x, y) in enumerate(pairs)]
    for copy in copies:
        copy.start()
    for rel in range(ROWS):
        if rel % 8 == 0:
            copies[rel // 8].wait()
        ref = s_ref if rel < 8 else q_ref
        start = pl.multiple_of(tbl_ref[rel] * NO, NO)
        for kt in range(KT):
            g, place = (kt // 4, kt % 4) if kt < CB else (kt - CB, 4)
            hi, lo = split(ref[rel % 8, kt])
            ghi[g, pl.ds(start, NO), place * 128 : (place + 1) * 128] = hi
            ghi[g, pl.ds(start, NO), 640 + place * 128 : 640 + (place + 1) * 128] = hi
            glo[g, pl.ds(start, NO), place * 128 : (place + 1) * 128] = lo
    copies[2].wait()
    chi = jnp.zeros((NO * NO, NO), jnp.float32)
    for g in range(5):
        parts = [k_ref[g * 4 + cc, :, 0:128] for cc in range(4)]
        parts.append(
            jnp.concatenate([k_ref[g * 4 + cc, :, 128:NV] for cc in range(4)], axis=1)
        )
        hi, lo = split(jnp.concatenate(parts, axis=1))
        chi = chi + dot_nt(ghi[g, :, 0:640], hi) + dot_nt(ghi[g, :, 0:640], lo)
        chi = chi + dot_nt(glo[g], hi)
    chi_ref[...] = chi.T


def dot_nt(x, y):
    return lax.dot_general(x, y, NT, preferred_element_type=jnp.float32)


def prepare(tbl, s, q, k):
    return pl.pallas_call(
        prepare_kernel,
        out_shape=(
            pltpu.VMEM((5, NO * NO, 1280), jnp.bfloat16),
            pltpu.VMEM((5, NO * NO, 640), jnp.bfloat16),
            jax.ShapeDtypeStruct((NO, NO * NO), jnp.float32),
        ),
        in_specs=[pl.BlockSpec(memory_space=pltpu.SMEM)]
        + [pl.BlockSpec(memory_space=pltpu.HBM)] * 3,
        out_specs=(VMEM, VMEM, VMEM),
        scratch_shapes=[
            pltpu.VMEM((8, KT, NO, 128), jnp.float32),
            pltpu.VMEM((8, KT, NO, 128), jnp.float32),
            pltpu.VMEM((CB, NO, NV), jnp.float32),
            pltpu.SemaphoreType.DMA((3,)),
        ],
        compiler_params=pltpu.CompilerParams(vmem_limit_bytes=11 << 20),
        cost_estimate=pl.CostEstimate(flops=0, bytes_accessed=8 << 20, transcendentals=0),
    )(tbl, s, q, k)


def ladder_kernel(group, ghi, glo, ready, *refs):
    out = refs[-1]
    total = dot_nt(ready[...], ghi[group]) + dot_nt(ready[:, 0:640], glo[group])
    if group > 0:
        total = total + refs[0][...]
    if group < 4:
        out[...] = total
        return
    for a in range(AB):
        for c in range(COLS):
            start = a * NV + c * CB
            out[c, a * CB : (a + 1) * CB, :] = total[start : start + CB, :]


def ladder(ghi, glo, source, group, before=None):
    operands = [ghi, glo, source]
    if group > 0:
        operands.append(before)
    if group == 4:
        shape = (COLS, AB * CB, NO * NO)
        out_shape = pltpu.HBM(shape, jnp.float32)
        out_specs = pl.BlockSpec(shape, lambda: (0, 0, 0))
    else:
        out_shape = pltpu.VMEM((VROWS, NO * NO), jnp.float32)
        out_specs = VMEM
    return pl.pallas_call(
        functools.partial(ladder_kernel, group),
        out_shape=out_shape,
        in_specs=[VMEM] * len(operands),
        out_specs=out_specs,
        compiler_params=pltpu.CompilerParams(vmem_limit_bytes=11 << 20),
        cost_estimate=pl.CostEstimate(
            flops=3 * 2 * 1600 * 640 * 256, bytes_accessed=8 << 20, transcendentals=0
        ),
    )(*operands)


def block_kernel(ghi, glo, e_ref, p_ref):
    for g in range(5):
        block = dot_nt(e_ref[...], ghi[g, :, 0:640]) + dot_nt(e_ref[...], glo[g])
        for a in range(AB):
            row = a * CB + g * 4
            p_ref[row : row + 4, :] = block[a * 4 : a * 4 + 4, :]


def own_block(ghi, glo, onehot):
    return pl.pallas_call(
        block_kernel,
        out_shape=jax.ShapeDtypeStruct((AB * CB, NO * NO), jnp.float32),
        in_specs=[VMEM] * 3,
        out_specs=VMEM,
        compiler_params=pltpu.CompilerParams(vmem_limit_bytes=4 << 20),
        cost_estimate=pl.CostEstimate(flops=1 << 31, bytes_accessed=6 << 20, transcendentals=0),
    )(ghi, glo, onehot)


def post_kernel(tbl_ref, x_ref, chi_ref, w_ref, f_ref, p_ref, o_ref, c0, c1, r0, r1, m1):
    owner = lax.broadcasted_iota(jnp.int32, (NO, NO * NO), 1) // NO
    for rel in range(ROWS):
        k = tbl_ref[rel]
        piece = chi_ref[rel] + w_ref[pl.ds(pl.multiple_of(k * NO, NO), NO), :]
        piece = piece - jnp.where(owner == k, f_ref[...], 0.0)
        c0[pl.ds(k, NO, stride=NO), :] = piece[:, 0:128]
        c1[pl.ds(k, NO, stride=NO), :] = piece[:, 128:256]
    chi = jnp.concatenate([c0[...], c1[...]], axis=1)
    total = x_ref[0]
    for c in range(1, COLS):
        total = total + x_ref[c]
    total = total + jnp.dot(
        p_ref[...], chi, precision=lax.Precision.HIGHEST, preferred_element_type=jnp.float32
    )
    total = jnp.concatenate([total, jnp.zeros((256 - AB * CB, NO * NO), jnp.float32)], axis=0)
    raw = total.T
    r0[...] = raw[:, 0:128]
    r1[...] = raw[:, 128:256]
    for i in range(NO):
        m1[i * NO : (i + 1) * NO, 0:128] = r0[pl.ds(i, NO, stride=NO), :]
        m1[i * NO : (i + 1) * NO, 128:256] = r1[pl.ds(i, NO, stride=NO), :]
    flipped = m1[...]
    for d in range(ROWS * COLS):
        o_ref[d, 0:2, :] = raw[2 * d : 2 * d + 2, :]
        o_ref[d, 2:4, :] = flipped[2 * d : 2 * d + 2, :]


def post(tbl, scattered, chi, bare, fock, block):
    return pl.pallas_call(
        post_kernel,
        out_shape=jax.ShapeDtypeStruct((ROWS * COLS, 4, 256), jnp.float32),
        in_specs=[pl.BlockSpec(memory_space=pltpu.SMEM)] + [VMEM] * 5,
        out_specs=VMEM,
        scratch_shapes=[pltpu.VMEM((NO * NO, 128), jnp.float32)] * 4
        + [pltpu.VMEM((NO * NO, 256), jnp.float32)],
        compiler_params=pltpu.CompilerParams(vmem_limit_bytes=12 << 20),
        cost_estimate=pl.CostEstimate(
            flops=6 * 2 * 200 * 65536, bytes_accessed=3 << 20, transcendentals=0
        ),
    )(tbl, scattered, chi, bare, fock, block)


def final_kernel(e_ref, x_ref, tf_ref, vrow_ref, vcol_ref, o_ref, left, right):
    for o in range(2):
        for s in range(2):
            for a in range(AB):
                pieces = [x_ref[o, s, c, :, a * CB : (a + 1) * CB] for c in range(COLS)]
                line = jnp.concatenate(pieces, axis=1)
                left[o, s, pl.ds(a, ROWS, stride=AB), :] = line[:, 0:128]
                right[o, s, pl.ds(a, ROWS, stride=AB), 0:32] = line[:, 128:NV]
    for s in range(2):
        full = [
            jnp.concatenate([left[o, s], right[o, s, :, 0:32]], axis=1) for o in range(2)
        ]
        total = full[0] + full[1].T + tf_ref[s]
        den = (e_ref[s] - vcol_ref[...]) - vrow_ref[...]
        o_ref[s] = total / den


def finish(e, x, tf, eps_vir):
    return pl.pallas_call(
        final_kernel,
        out_shape=jax.ShapeDtypeStruct((2, NV, NV), jnp.float32),
        in_specs=[pl.BlockSpec(memory_space=pltpu.SMEM)]
        + [pl.BlockSpec(memory_space=pltpu.VMEM)] * 4,
        out_specs=pl.BlockSpec(memory_space=pltpu.VMEM),
        scratch_shapes=[pltpu.VMEM((2, 2, NV, 128), jnp.float32)] * 2,
        cost_estimate=pl.CostEstimate(flops=0, bytes_accessed=2 << 20, transcendentals=0),
    )(e, x, tf, eps_vir.reshape(1, NV), eps_vir.reshape(NV, 1))


def on_device(amplitudes, vvvv, hole_ints, exchange_ints, fock_occ, fock_vir, eps_occ, eps_vir):
    high = lax.Precision.HIGHEST
    row = lax.axis_index("row")
    col = lax.axis_index("col")
    t = amplitudes[0]
    packed = pack(t)
    arrived = lax.all_to_all(packed, "col", split_axis=0, concat_axis=0, tiled=True)
    v4 = pltpu.with_memory_space_constraint(vvvv.transpose(0, 2, 1, 3), pltpu.HBM)
    arrived, zero = lax.optimization_barrier((arrived, split_integrals(v4, 0)))
    x = arrived.reshape(NO, KT, 128).transpose(1, 0, 2)

    def hop(value, dy, dz, dc):
        return lax.ppermute(value, "row", row_perm(dy, dz, dc))

    k4 = exchange_ints[0].transpose(1, 0, 2)
    pair = jnp.stack([x, hop(x, 1, 0, 0)])
    pair, opening = lax.optimization_barrier((pair, split_integrals(v4, 1)))
    ahead = hop(pair, 0, 1, 0)
    behind = hop(pair, 0, 3, 0)
    ahead, behind, second = lax.optimization_barrier((ahead, behind, split_integrals(v4, 2)))
    far = [hop(ahead[0], 0, 1, 0), hop(behind[1], 0, 3, 0)]
    far, third = lax.optimization_barrier((far, split_integrals(v4, 3)))
    far = jnp.stack(far)
    own = jnp.stack([pair, ahead, far, behind])
    other = hop(own, 0, 0, 1)
    fourth = split_integrals(v4, 4)
    own = own.reshape(8, KT, NO, 128)
    other = other.reshape(8, KT, NO, 128)

    rel = jnp.arange(ROWS, dtype=jnp.int32)
    dc, dz, dy = rel // 8, (rel // 2) % 4, rel % 2
    table = ((row // 8 + dy) % 2) * 8 + ((row // 2 + dz) % 4) * 2 + ((row % 2) ^ dc)

    e_row = jnp.arange(EROWS, dtype=jnp.int32)[:, None]
    e_col = jnp.arange(640, dtype=jnp.int32)[None, :]
    want = row * AB + e_row // 4
    cc = e_row % 4
    place = jnp.where(want < 128, cc * 128 + want, 512 + cc * 32 + want - 128)
    onehot = (e_col == place).astype(jnp.bfloat16)

    hbm = lambda value: pltpu.with_memory_space_constraint(value, pltpu.HBM)
    ghi, glo, chi = prepare(table, hbm(own), hbm(other), hbm(k4))

    def fold(value, flip):
        return value + lax.ppermute(value, "col", [(c, c ^ flip) for c in range(COLS)])

    chi = fold(chi, 1)
    lad = ladder(ghi, glo, zero, 0)
    chi = fold(chi, 2)
    lad = ladder(ghi, glo, opening, 1, before=lad)
    lad = ladder(ghi, glo, second, 2, before=lad)
    chi = fold(chi, 4)
    lad = ladder(ghi, glo, third, 3, before=lad)
    chi = jnp.stack([chi, hop(chi, 1, 0, 0)])
    lad = ladder(ghi, glo, fourth, 4, before=lad)
    lad, chi, holes = lax.optimization_barrier((lad, chi, hole_ints))
    scattered = lax.all_to_all(lad, "col", split_axis=0, concat_axis=0, tiled=True)

    chi = jnp.stack([chi] + [hop(chi, 0, dz, 0) for dz in (1, 2, 3)])
    chi = jnp.stack([chi, hop(chi, 0, 0, 1)]).reshape(ROWS, NO, NO * NO)
    block = own_block(ghi, glo, onehot)
    bare = holes.reshape(NO * NO, NO * NO)
    fock = jnp.tile(fock_occ, (1, NO))
    sending = post(table, scattered, chi, bare, fock, block)
    back = lax.all_to_all(sending, ("row", "col"), split_axis=0, concat_axis=0, tiled=True)
    back = back.reshape(ROWS, COLS, 2, 2, 256).transpose(2, 3, 1, 0, 4)

    tf = jnp.einsum("jac,cb->jab", t, fock_vir, precision=high)
    tf = tf + jnp.einsum("ac,jcb->jab", fock_vir, t, precision=high)
    first = lax.dynamic_slice_in_dim(eps_occ, row, 1)
    second = lax.dynamic_slice_in_dim(eps_occ, col * 2, 2)
    return finish(first + second, back, tf, eps_vir)[None]


def solution(mesh):
    in_specs = (
        P("row", "col", None, None),
        P("row", None, "col", None),
        P(),
        P("row", None, "col", None),
        P(),
        P(),
        P(),
        P(),
    )
    return jax.shard_map(
        on_device,
        mesh=mesh,
        in_specs=in_specs,
        out_specs=P("row", "col", None, None),
        check_vma=False,
    )
```
